512 devices in a mesh: modes: 256 (over y, z, x), grp: 2 (over core).
Axes of the slice: x: 4, y: 8, z: 8, core: 2. Of those that a mesh axis runs over, the one named last changes fastest.
Arguments:
- left_core: bfloat16 [524288, 512], P(('modes', 'grp')), may hold values from -6 to 6
- right_core: bfloat16 [524288, 512], P(('modes', 'grp')), may hold values from -6 to 6
- gauss_core: bfloat16 [524288, 256], P(('modes', 'grp')), may hold values from -0.0078125 to 0.0078125
Outputs:
- left_new: bfloat16 [524288, 256], P(('modes', 'grp'))
- right_new: bfloat16 [524288, 256], P(('modes', 'grp'))
The draws below stay inside these ranges and needn't reach their ends.
All inputs are finite; a program needn't handle non-finite values.
Results may differ from the reference program's by a relative error of at most 0.0012.
Values sent between devices are 32-bit elements; how exact they have to be, the bound alone decides.
No kernel may reach another device: no remote copies, remote signals or barrier semaphores. Data moves between devices by JAX's collectives and lax.ppermute only.
A program may use at most 64 MiB of HBM per device.

```python
import math
import jax
import jax.numpy as jnp
from jax import lax

R = 512
K = 256
ROWS = 524288


def levels(key, dims, pieces, low, high):
    level, own = 1.0, jax.random.fold_in(key, 6)
    for dim, shards_of in pieces:
        steps = jnp.exp(jax.random.uniform(jax.random.fold_in(own, dim), (shards_of,), jnp.float32, low / len(pieces), high / len(pieces)))
        level = level * jnp.repeat(steps, dims[dim] // shards_of).reshape([-1 if axis == dim else 1 for axis in range(len(dims))])
    return level


def centred(rng, dims, deviation, reach, pieces=(), dtype=jnp.bfloat16):
    result = jax.random.normal(rng, dims, jnp.float32) * deviation
    if len(pieces) > 0:
        result = levels(rng, dims, pieces, -0.22, 0.18) * result
    return jnp.clip(result, min=-reach, max=reach).astype(dtype)


def setup_inputs(seed: int = 0) -> dict:
    splits = jax.random.split(jax.random.key(seed), 4)
    left_core = centred(splits[0], (ROWS, R), 1.0, 6.0, ((0, 512),))
    right_core = centred(splits[1], (ROWS, R), 1.0, 6.0, ((0, 512),))
    gauss_core = centred(splits[2], (ROWS, K), ROWS ** -0.5, 0.0078125, ((0, 512),))
    return {"left_core": left_core, "right_core": right_core, "gauss_core": gauss_core}


def reference(left_core, right_core, gauss_core):
    high = lax.Precision.HIGHEST
    sketch = lax.dot_general(right_core.astype(jnp.float32), gauss_core.astype(jnp.float32), (((0,), (0,)), ((), ())), preferred_element_type=jnp.float32)
    tall_sketch = jnp.dot(left_core.astype(jnp.float32), sketch, precision=high)
    gram = lax.dot_general(tall_sketch, tall_sketch, (((0,), (0,)), ((), ())), precision=high)
    chol_lower = jnp.linalg.cholesky(gram)
    q_trans = jax.scipy.linalg.solve_triangular(chol_lower, tall_sketch.T, lower=True)
    projected = jnp.dot(q_trans, left_core.astype(jnp.float32), precision=high)
    norm_scale = math.sqrt(ROWS)
    left_new = (q_trans.T * norm_scale).astype(jnp.bfloat16)
    right_new = jnp.dot(right_core.astype(jnp.float32), (projected / norm_scale).T, precision=high).astype(jnp.bfloat16)
    return (left_new, right_new)
```

```python
import math

import jax
import jax.numpy as jnp
from jax import lax
from jax.experimental import pallas as pl
from jax.experimental.pallas import tpu as pltpu
from jax.sharding import Mesh
from jax.sharding import PartitionSpec as P

GRID = ("modes_0", "modes_1", "modes_2", "grp")
PLANE = ("modes_1", "modes_2")
HI = lax.Precision.HIGHEST
F32, BF16 = jnp.float32, jnp.bfloat16
T = 128
SUB = 8
ANY = pl.BlockSpec(memory_space=pl.ANY)
VMEM = pl.BlockSpec(memory_space=pltpu.VMEM)
SMEM = pl.BlockSpec(memory_space=pltpu.SMEM)


def dot(x, y, dims=((1,), (0,)), precision=HI):
    return lax.dot_general(x, y, (dims, ((), ())), precision=precision, preferred_element_type=F32)


def tiles_of(rank, target):
    sketch = [("s", i, j) for j in range(target // T) for i in range(rank // T)]
    gram = [("g", i, j) for j in range(rank // T) for i in range(j, rank // T)]
    both = sketch + gram
    return both[: len(both) // 2], both[len(both) // 2 :]


def local_products(core_ref, left_hbm, right_hbm, gauss_hbm, keep_ref, send_ref, left, right, gauss, sems):
    copies = [
        pltpu.make_async_copy(src, dst, sems.at[i])
        for i, (src, dst) in enumerate(((right_hbm, right), (gauss_hbm, gauss), (left_hbm, left)))
    ]
    for copy in copies:
        copy.start()
    rank, target = right.shape[1], gauss.shape[1]
    halves = tiles_of(rank, target)
    core = core_ref[0]

    def put(kind, col, value, first):
        for i in range(value.shape[0] // T):
            tile = (kind, first + i, col)
            half = 0 if tile in halves[0] else 1
            place = halves[half].index(tile)
            block = value[i * T : (i + 1) * T, :]

            @pl.when(core == half)
            def _():
                keep_ref[place] = block

            @pl.when(core != half)
            def _():
                send_ref[place] = block

    copies[0].wait()
    copies[1].wait()
    x = dot(right[...], gauss[...], ((0,), (0,)), None)
    for j in range(target // T):
        put("s", j, x[:, j * T : (j + 1) * T], 0)
    copies[2].wait()
    for j in range(0, rank // T, 2):
        y = dot(left[:, j * T :], left[:, j * T : (j + 2) * T], ((0,), (0,)), None)
        put("g", j, y[:, :T], j)
        put("g", j + 1, y[T:, T:], j + 1)


def products(core, left_core, right_core, gauss_core):
    rank, target = right_core.shape[1], gauss_core.shape[1]
    half = jax.ShapeDtypeStruct((len(tiles_of(rank, target)[0]), T, T), F32)
    return pl.pallas_call(
        local_products,
        out_shape=(half, half),
        in_specs=[SMEM, ANY, ANY, ANY],
        out_specs=[VMEM, VMEM],
        scratch_shapes=[
            pltpu.VMEM(left_core.shape, BF16),
            pltpu.VMEM(right_core.shape, BF16),
            pltpu.VMEM(gauss_core.shape, BF16),
            pltpu.SemaphoreType.DMA((3,)),
        ],
        name="products",
    )(core, left_core, right_core, gauss_core)


def lane_of(x, c):
    return jnp.take_along_axis(x, jnp.full(x.shape, c, jnp.int32), axis=1)


def row_of(x, k):
    return lax.broadcast_in_dim(x[k : k + 1, :], x.shape, (0, 1))


def inverse_factor_of_tile(a):
    lane = lax.broadcasted_iota(jnp.int32, (SUB, T), 1)
    sub = lax.broadcasted_iota(jnp.int32, (SUB, T), 0)
    rows = [a[SUB * i : SUB * (i + 1), :] for i in range(T // SUB)]
    out = []
    for s in range(T // SUB):
        base = SUB * s
        own = (lane >= base) & (lane < base + SUB)
        w = rows[s]
        cols = [lane_of(w, base + k) for k in range(SUB)]
        w = jnp.where(own, jnp.where(lane == sub + base, 1.0, 0.0), w)
        f = jnp.zeros((SUB, T), F32)
        for k in range(SUB):
            here = sub == k
            pivot = row_of(cols[k], k)
            inverse = 1.0 / pivot
            row = row_of(w, k)
            f = jnp.where(here, row * lax.rsqrt(pivot), f)
            for j in range(k + 1, SUB):
                t = row_of(cols[j], k) * inverse
                cols[j] = jnp.where(here, t, cols[j] - cols[k] * t)
            t = row * inverse
            w = jnp.where(here, t, w - cols[k] * t)
        out.append(jnp.where(lane <= sub + base, f, 0.0))
        ws = [row_of(w, k) for k in range(SUB)]
        for i in range(s + 1, T // SUB):
            r = rows[i]
            m = [lane_of(r, base + k) for k in range(SUB)]
            r = jnp.where(own, 0.0, r)
            for k in range(SUB):
                r = r - m[k] * ws[k]
            rows[i] = r
    return jnp.concatenate(out, 0)


def split(x):
    high = x.astype(BF16)
    return high, (x - high.astype(F32)).astype(BF16)


def truncate(norm, core_ref, mine_ref, theirs_ref, left_hbm, right_hbm, left_new_ref, right_new_ref,
             left, right, tiles, sketch, gram_left, sems):
    copies = [
        pltpu.make_async_copy(left_hbm, left, sems.at[0]),
        pltpu.make_async_copy(right_hbm, right, sems.at[1]),
    ]
    for copy in copies:
        copy.start()
    core = core_ref[0]
    tiles[core] = mine_ref[...]
    tiles[1 - core] = theirs_ref[...]
    rank, target = sketch.shape
    for half, held in enumerate(tiles_of(rank, target)):
        for place, (kind, i, j) in enumerate(held):
            tile = tiles[half, place]
            if kind == "s":
                sketch[i * T : (i + 1) * T, j * T : (j + 1) * T] = tile
            else:
                gram_left[i * T : (i + 1) * T, j * T : (j + 1) * T] = tile
                if i != j:
                    gram_left[j * T : (j + 1) * T, i * T : (i + 1) * T] = tile.T
    s = sketch[...]
    cross = dot(gram_left[...], s)
    gram = dot(s, cross, ((0,), (0,)))
    m11 = inverse_factor_of_tile(gram[:T, :T])
    u12 = dot(m11, gram[:T, T:])
    m22 = inverse_factor_of_tile(gram[T:, T:] - dot(u12, u12, ((0,), (0,))))
    m21 = -dot(m22, dot(u12, m11, ((0,), (0,))))
    m = jnp.concatenate(
        [jnp.concatenate([m11, jnp.zeros_like(m11)], 1), jnp.concatenate([m21, m22], 1)], 0
    )
    for scale, factor, copy, held, out_ref in (
        (norm, s, copies[0], left, left_new_ref),
        (1.0 / norm, cross, copies[1], right, right_new_ref),
    ):
        high, low = split(dot(factor, m, ((1,), (1,))) * scale)
        copy.wait()
        x = held[...]
        out_ref[...] = (dot(x, high, precision=None) + dot(x, low, precision=None)).astype(BF16)


def truncated(norm, core, mine, theirs, left_core, right_core, target):
    rows, rank = left_core.shape
    import functools
    out = jax.ShapeDtypeStruct((rows, target), BF16)
    return pl.pallas_call(
        functools.partial(truncate, norm),
        out_shape=(out, out),
        in_specs=[SMEM, VMEM, VMEM, ANY, ANY],
        out_specs=[VMEM, VMEM],
        scratch_shapes=[
            pltpu.VMEM(left_core.shape, BF16),
            pltpu.VMEM(right_core.shape, BF16),
            pltpu.VMEM((2, *mine.shape), F32),
            pltpu.VMEM((rank, target), F32),
            pltpu.VMEM((rank, rank), F32),
            pltpu.SemaphoreType.DMA((2,)),
        ],
        name="truncate",
    )(core, mine, theirs, left_core, right_core)


def to_all(x, axes, count):
    return lax.all_to_all(jnp.broadcast_to(x, (count, *x.shape)), axes, 0, 0, tiled=True)


def local(left_core, right_core, gauss_core):
    devices = math.prod(lax.axis_size(a) for a in GRID)
    plane = lax.axis_size(PLANE[0]) * lax.axis_size(PLANE[1])
    norm = math.sqrt(left_core.shape[0] * devices)
    core = lax.axis_index("grp").reshape(1)
    swap = [(0, 1), (1, 0)]
    keep, send = products(core, left_core, right_core, gauss_core)
    x = keep + lax.ppermute(send, "grp", swap)
    x = lax.all_to_all(x.reshape(plane, -1, 4, T), PLANE, 0, 0, tiled=True).sum(0)
    x = to_all(x, "modes_0", lax.axis_size("modes_0")).reshape(-1, *x.shape).sum(0)
    mine = to_all(x, PLANE, plane).reshape(keep.shape)
    theirs = lax.ppermute(mine, "grp", swap)
    return truncated(norm, core, mine, theirs, left_core, right_core, gauss_core.shape[1])


def solution(mesh):
    finer = Mesh(mesh.devices.reshape(8, 8, 4, mesh.shape["grp"]), GRID)
    spec = P(GRID, None)
    return jax.shard_map(
        local, mesh=finer, in_specs=(spec, spec, spec), out_specs=(spec, spec), check_vma=False
    )
```

```python
import functools
import math

import jax
import jax.numpy as jnp
from jax import lax
from jax.experimental import pallas as pl
from jax.experimental.pallas import tpu as pltpu
from jax.sharding import Mesh
from jax.sharding import PartitionSpec as P

GRID = ("modes_0", "modes_1", "modes_2", "grp")
PLANE = ("modes_1", "modes_2")
HI = lax.Precision.HIGHEST
F32, BF16 = jnp.float32, jnp.bfloat16
T = 128
SUB = 8
OUTER = 32
ANY = pl.BlockSpec(memory_space=pl.ANY)
VMEM = pl.BlockSpec(memory_space=pltpu.VMEM)
SMEM = pl.BlockSpec(memory_space=pltpu.SMEM)


def dot(x, y, dims=((1,), (0,)), precision=HI):
    return lax.dot_general(x, y, (dims, ((), ())), precision=precision, preferred_element_type=F32)


def tiles_of(rank, target):
    sketch = [("s", i, j) for j in range(target // T) for i in range(rank // T)]
    gram = [("g", i, j) for j in range(rank // T) for i in range(j, rank // T)]
    both = sketch + gram
    return both[: len(both) // 2], both[len(both) // 2 :]


def local_products(core_ref, left_hbm, right_hbm, gauss_hbm, keep_ref, send_ref, left, right, gauss, sems):
    copies = [
        pltpu.make_async_copy(src, dst, sems.at[i])
        for i, (src, dst) in enumerate(((right_hbm, right), (gauss_hbm, gauss), (left_hbm, left)))
    ]
    for copy in copies:
        copy.start()
    rank, target = right.shape[1], gauss.shape[1]
    halves = tiles_of(rank, target)
    core = core_ref[0]

    def put(kind, col, value, first):
        for i in range(value.shape[0] // T):
            tile = (kind, first + i, col)
            half = 0 if tile in halves[0] else 1
            place = halves[half].index(tile)
            block = value[i * T : (i + 1) * T, :]

            @pl.when(core == half)
            def _():
                keep_ref[place] = block

            @pl.when(core != half)
            def _():
                send_ref[place] = block

    copies[0].wait()
    copies[1].wait()
    x = dot(right[...], gauss[...], ((0,), (0,)), None)
    for j in range(target // T):
        put("s", j, x[:, j * T : (j + 1) * T], 0)
    copies[2].wait()
    for j in range(0, rank // T, 2):
        y = dot(left[:, j * T :], left[:, j * T : (j + 2) * T], ((0,), (0,)), None)
        put("g", j, y[:, :T], j)
        put("g", j + 1, y[T:, T:], j + 1)


def products(core, left_core, right_core, gauss_core):
    rank, target = right_core.shape[1], gauss_core.shape[1]
    half = pltpu.VMEM((len(tiles_of(rank, target)[0]), T, T), F32)
    return pl.pallas_call(
        local_products,
        out_shape=(half, half),
        in_specs=[SMEM, ANY, ANY, ANY],
        out_specs=[VMEM, VMEM],
        scratch_shapes=[
            pltpu.VMEM(left_core.shape, BF16),
            pltpu.VMEM(right_core.shape, BF16),
            pltpu.VMEM(gauss_core.shape, BF16),
            pltpu.SemaphoreType.DMA((3,)),
        ],
        name="products",
    )(core, left_core, right_core, gauss_core)


def lane_of(x, c):
    x = x[c // T]
    return jnp.take_along_axis(x, jnp.full(x.shape, c % T, jnp.int32), axis=1)


def row_of(x, k):
    return lax.broadcast_in_dim(x[k : k + 1, :], x.shape, (0, 1))


def tree_sum(terms):
    while len(terms) > 1:
        rest = terms[len(terms) // 2 * 2 :]
        terms = [x + y for x, y in zip(terms[::2], terms[1::2])] + rest
    return terms[0]


def split(x):
    high = x.astype(BF16)
    return high, (x - high.astype(F32)).astype(BF16)


def dot_split(x, y, dims=((1,), (0,))):
    (xh, xl), (yh, yl) = x, y
    return dot(xh, yh, dims, None) + (dot(xh, yl, dims, None) + dot(xl, yh, dims, None))


def inverse_factor(a):
    n = a.shape[0]
    parts = range(n // T)
    sub = lax.broadcasted_iota(jnp.int32, (SUB, T), 0)
    lanes = [lax.broadcasted_iota(jnp.int32, (SUB, T), 1) + T * h for h in parts]
    done = []
    for first in range(0, n, OUTER):
        block = a[first : first + OUTER, :]
        if first:
            u = jnp.concatenate(done, 0)
            row = lax.broadcasted_iota(jnp.int32, u.shape, 0)
            col = lax.broadcasted_iota(jnp.int32, u.shape, 1)
            x = dot_split(
                split(u[:, first : first + OUTER]),
                split(jnp.where((col <= row) | (col >= first), u, 0.0)),
                ((0,), (0,)),
            )
            col = lax.broadcasted_iota(jnp.int32, block.shape, 1)
            block = jnp.where(col >= first, block, 0.0) - x
        rows = [
            [block[i : i + SUB, T * h : T * (h + 1)] for h in parts] for i in range(0, OUTER, SUB)
        ]
        for s in range(OUTER // SUB):
            base = first + SUB * s
            here_part = base // T
            lane = lanes[here_part]
            own = (lane >= base) & (lane < base + SUB)
            w = list(rows[s])
            cols = [lane_of(w, base + k) for k in range(SUB)]
            w[here_part] = jnp.where(
                own, jnp.where(lane == sub + base, 1.0, 0.0), w[here_part]
            )
            f = [jnp.zeros((SUB, T), F32)] * len(w)
            pivot = row_of(cols[0], 0)
            for k in range(SUB):
                here = sub == k
                inverse, root = 1.0 / pivot, lax.rsqrt(pivot)
                for j in range(k + 1, SUB):
                    r = row_of(cols[j], k)
                    if j == k + 1:
                        rest = cols[j] - (cols[k] * r) * inverse
                        pivot = row_of(rest, j)
                        cols[j] = jnp.where(here, r * inverse, rest)
                    else:
                        t = r * inverse
                        cols[j] = jnp.where(here, t, cols[j] - cols[k] * t)
                for h in parts:
                    r = row_of(w[h], k)
                    f[h] = jnp.where(here, r * root, f[h])
                    t = r * inverse
                    w[h] = jnp.where(here, t, w[h] - cols[k] * t)
            keep = [(lanes[h] <= sub + base) | (lanes[h] >= first + OUTER) for h in parts]
            done.append(jnp.concatenate([jnp.where(keep[h], f[h], 0.0) for h in parts], 1))
            ws = [[row_of(w[h], k) for k in range(SUB)] for h in parts]
            for i in range(s + 1, OUTER // SUB):
                m = [lane_of(rows[i], base + k) for k in range(SUB)]
                r = list(rows[i])
                r[here_part] = jnp.where(own, 0.0, r[here_part])
                rows[i] = [r[h] - tree_sum([x * y for x, y in zip(m, ws[h])]) for h in parts]
    m = jnp.concatenate(done, 0)
    row = lax.broadcasted_iota(jnp.int32, m.shape, 0)
    col = lax.broadcasted_iota(jnp.int32, m.shape, 1)
    return jnp.where(row >= col, m, 0.0)


def truncate(norm, core_ref, mine_ref, theirs_ref, left_hbm, right_hbm, left_new_ref, right_new_ref,
             left, right, sketch, gram_left, tile_sems, sems):
    rank, target = sketch.shape
    halves = tiles_of(rank, target)
    core = core_ref[0]

    def place(half, i):
        kind, row, col = halves[half][i]
        ref = sketch if kind == "s" else gram_left
        return ref.at[pl.ds(row * T, T), pl.ds(col * T, T)]

    for own in range(2):

        @pl.when(core == own)
        def _():
            for half in range(2):
                src = mine_ref if half == own else theirs_ref
                for i in range(len(halves[half])):
                    pltpu.make_async_copy(src.at[i], place(half, i), tile_sems.at[half, i]).start()

    copies = [
        pltpu.make_async_copy(left_hbm, left, sems.at[0]),
        pltpu.make_async_copy(right_hbm, right, sems.at[1]),
    ]
    for copy in copies:
        copy.start()
    for half in range(2):
        for i in range(len(halves[half])):
            pltpu.make_async_copy(mine_ref.at[i], place(half, i), tile_sems.at[half, i]).wait()
    for i in range(rank // T):
        for j in range(i):
            tile = gram_left[i * T : (i + 1) * T, j * T : (j + 1) * T]
            gram_left[j * T : (j + 1) * T, i * T : (i + 1) * T] = tile.T
    s = split(sketch[...])
    cross = split(dot_split(split(gram_left[...]), s))
    gram = dot_split(s, cross, ((0,), (0,)))
    for copy in copies:
        copy.wait()
    tall = [
        split(dot(held[...], high, precision=None) + dot(held[...], low, precision=None))
        for held, (high, low) in ((left, s), (right, cross))
    ]
    m = split(inverse_factor(gram))
    left_new_ref[...] = (dot_split(tall[0], m, ((1,), (1,))) * norm).astype(BF16)
    right_new_ref[...] = (dot_split(tall[1], m, ((1,), (1,))) * (1.0 / norm)).astype(BF16)


def truncated(norm, core, mine, theirs, left_core, right_core, target):
    rows, rank = left_core.shape
    out = jax.ShapeDtypeStruct((rows, target), BF16)
    return pl.pallas_call(
        functools.partial(truncate, norm),
        out_shape=(out, out),
        in_specs=[SMEM, ANY, ANY, ANY, ANY],
        out_specs=[VMEM, VMEM],
        scratch_shapes=[
            pltpu.VMEM(left_core.shape, BF16),
            pltpu.VMEM(right_core.shape, BF16),
            pltpu.VMEM((rank, target), F32),
            pltpu.VMEM((rank, rank), F32),
            pltpu.SemaphoreType.DMA((2, mine.shape[0])),
            pltpu.SemaphoreType.DMA((2,)),
        ],
        compiler_params=pltpu.CompilerParams(vmem_limit_bytes=40 << 20),
        name="truncate",
    )(core, mine, theirs, left_core, right_core)


def to_all(x, axes, count):
    return lax.all_to_all(jnp.broadcast_to(x, (count, *x.shape)), axes, 0, 0, tiled=True)


def local(left_core, right_core, gauss_core):
    devices = math.prod(lax.axis_size(a) for a in GRID)
    plane = lax.axis_size(PLANE[0]) * lax.axis_size(PLANE[1])
    norm = math.sqrt(left_core.shape[0] * devices)
    core = lax.axis_index("grp").reshape(1)
    swap = [(0, 1), (1, 0)]
    keep, send = products(core, left_core, right_core, gauss_core)
    x = keep + lax.ppermute(send, "grp", swap)
    x = lax.all_to_all(x.reshape(plane, -1, 4, T), PLANE, 0, 0, tiled=True).sum(0)
    x = to_all(x, "modes_0", lax.axis_size("modes_0")).reshape(-1, *x.shape).sum(0)
    mine = to_all(x, PLANE, plane).reshape(keep.shape)
    theirs = lax.ppermute(mine, "grp", swap)
    return truncated(norm, core, mine, theirs, left_core, right_core, gauss_core.shape[1])


def solution(mesh):
    finer = Mesh(mesh.devices.reshape(8, 8, 4, mesh.shape["grp"]), GRID)
    spec = P(GRID, None)
    return jax.shard_map(
        local, mesh=finer, in_specs=(spec, spec, spec), out_specs=(spec, spec), check_vma=False
    )
```

```python
import functools
import math

import jax
import jax.numpy as jnp
from jax import lax
from jax.experimental import pallas as pl
from jax.experimental.pallas import tpu as pltpu
from jax.sharding import Mesh
from jax.sharding import PartitionSpec as P

AXIS = "device"
CHIPS = (8, 8, 4)
HI = lax.Precision.HIGHEST
F32, BF16 = jnp.float32, jnp.bfloat16
T = 128
SUB = 8
OUTER = 32
ANY = pl.BlockSpec(memory_space=pl.ANY)
VMEM = pl.BlockSpec(memory_space=pltpu.VMEM)
SMEM = pl.BlockSpec(memory_space=pltpu.SMEM)


def dot(x, y, dims=((1,), (0,)), precision=HI):
    return lax.dot_general(x, y, (dims, ((), ())), precision=precision, preferred_element_type=F32)


def tiles_of(rank, target):
    sketch = [("s", i, j) for j in range(target // T) for i in range(rank // T)]
    gram = [("g", i, j) for j in range(rank // T) for i in range(j, rank // T)]
    both = sketch + gram
    return both[: len(both) // 2], both[len(both) // 2 :]


def local_products(core_ref, left_hbm, right_hbm, gauss_hbm, keep_ref, send_ref, left, right, gauss, sems):
    copies = [
        pltpu.make_async_copy(src, dst, sems.at[i])
        for i, (src, dst) in enumerate(((right_hbm, right), (gauss_hbm, gauss), (left_hbm, left)))
    ]
    for copy in copies:
        copy.start()
    rank, target = right.shape[1], gauss.shape[1]
    halves = tiles_of(rank, target)
    core = core_ref[0]

    def put(kind, col, value, first):
        for i in range(value.shape[0] // T):
            tile = (kind, first + i, col)
            half = 0 if tile in halves[0] else 1
            place = halves[half].index(tile)
            block = value[i * T : (i + 1) * T, :]

            @pl.when(core == half)
            def _():
                keep_ref[place] = block

            @pl.when(core != half)
            def _():
                send_ref[place] = block

    copies[0].wait()
    copies[1].wait()
    x = dot(right[...], gauss[...], ((0,), (0,)), None)
    for j in range(target // T):
        put("s", j, x[:, j * T : (j + 1) * T], 0)
    copies[2].wait()
    for j in range(0, rank // T, 2):
        y = dot(left[:, j * T :], left[:, j * T : (j + 2) * T], ((0,), (0,)), None)
        put("g", j, y[:, :T], j)
        put("g", j + 1, y[T:, T:], j + 1)


def products(core, left_core, right_core, gauss_core):
    rank, target = right_core.shape[1], gauss_core.shape[1]
    half = pltpu.VMEM((len(tiles_of(rank, target)[0]), T, T), F32)
    return pl.pallas_call(
        local_products,
        out_shape=(half, half),
        in_specs=[SMEM, ANY, ANY, ANY],
        out_specs=[VMEM, VMEM],
        scratch_shapes=[
            pltpu.VMEM(left_core.shape, BF16),
            pltpu.VMEM(right_core.shape, BF16),
            pltpu.VMEM(gauss_core.shape, BF16),
            pltpu.SemaphoreType.DMA((3,)),
        ],
        name="products",
    )(core, left_core, right_core, gauss_core)


def lane_of(x, c):
    x = x[c // T]
    return jnp.take_along_axis(x, jnp.full(x.shape, c % T, jnp.int32), axis=1)


def row_of(x, k):
    return lax.broadcast_in_dim(x[k : k + 1, :], x.shape, (0, 1))


def tree_sum(terms):
    while len(terms) > 1:
        rest = terms[len(terms) // 2 * 2 :]
        terms = [x + y for x, y in zip(terms[::2], terms[1::2])] + rest
    return terms[0]


def split(x):
    high = x.astype(BF16)
    return high, (x - high.astype(F32)).astype(BF16)


def dot_split(x, y, dims=((1,), (0,))):
    (xh, xl), (yh, yl) = x, y
    return dot(xh, yh, dims, None) + (dot(xh, yl, dims, None) + dot(xl, yh, dims, None))


def inverse_factor(a):
    n = a.shape[0]
    parts = range(n // T)
    sub = lax.broadcasted_iota(jnp.int32, (SUB, T), 0)
    lanes = [lax.broadcasted_iota(jnp.int32, (SUB, T), 1) + T * h for h in parts]
    done = []
    for first in range(0, n, OUTER):
        block = a[first : first + OUTER, :]
        if first:
            u = jnp.concatenate(done, 0)
            row = lax.broadcasted_iota(jnp.int32, u.shape, 0)
            col = lax.broadcasted_iota(jnp.int32, u.shape, 1)
            x = dot_split(
                split(u[:, first : first + OUTER]),
                split(jnp.where((col <= row) | (col >= first), u, 0.0)),
                ((0,), (0,)),
            )
            col = lax.broadcasted_iota(jnp.int32, block.shape, 1)
            block = jnp.where(col >= first, block, 0.0) - x
        rows = [
            [block[i : i + SUB, T * h : T * (h + 1)] for h in parts] for i in range(0, OUTER, SUB)
        ]
        for s in range(OUTER // SUB):
            base = first + SUB * s
            here_part = base // T
            lane = lanes[here_part]
            own = (lane >= base) & (lane < base + SUB)
            w = list(rows[s])
            cols = [lane_of(w, base + k) for k in range(SUB)]
            w[here_part] = jnp.where(
                own, jnp.where(lane == sub + base, 1.0, 0.0), w[here_part]
            )
            f = [jnp.zeros((SUB, T), F32)] * len(w)
            pivot = row_of(cols[0], 0)
            for k in range(SUB):
                here = sub == k
                inverse, root = 1.0 / pivot, lax.rsqrt(pivot)
                for j in range(k + 1, SUB):
                    r = row_of(cols[j], k)
                    if j == k + 1:
                        rest = cols[j] - (cols[k] * r) * inverse
                        pivot = row_of(rest, j)
                        cols[j] = jnp.where(here, r * inverse, rest)
                    else:
                        t = r * inverse
                        cols[j] = jnp.where(here, t, cols[j] - cols[k] * t)
                for h in parts:
                    r = row_of(w[h], k)
                    f[h] = jnp.where(here, r * root, f[h])
                    t = r * inverse
                    w[h] = jnp.where(here, t, w[h] - cols[k] * t)
            keep = [(lanes[h] <= sub + base) | (lanes[h] >= first + OUTER) for h in parts]
            done.append(jnp.concatenate([jnp.where(keep[h], f[h], 0.0) for h in parts], 1))
            ws = [[row_of(w[h], k) for k in range(SUB)] for h in parts]
            for i in range(s + 1, OUTER // SUB):
                m = [lane_of(rows[i], base + k) for k in range(SUB)]
                r = list(rows[i])
                r[here_part] = jnp.where(own, 0.0, r[here_part])
                rows[i] = [r[h] - tree_sum([x * y for x, y in zip(m, ws[h])]) for h in parts]
    m = jnp.concatenate(done, 0)
    row = lax.broadcasted_iota(jnp.int32, m.shape, 0)
    col = lax.broadcasted_iota(jnp.int32, m.shape, 1)
    return jnp.where(row >= col, m, 0.0)


def truncate(norm, core_ref, mine_ref, theirs_ref, left_hbm, right_hbm, left_new_ref, right_new_ref,
             left, right, sketch, gram_left, tile_sems, sems):
    rank, target = sketch.shape
    halves = tiles_of(rank, target)
    core = core_ref[0]

    def place(half, i):
        kind, row, col = halves[half][i]
        ref = sketch if kind == "s" else gram_left
        return ref.at[pl.ds(row * T, T), pl.ds(col * T, T)]

    for own in range(2):

        @pl.when(core == own)
        def _():
            for half in range(2):
                src = mine_ref if half == own else theirs_ref
                for i in range(len(halves[half])):
                    pltpu.make_async_copy(src.at[i], place(half, i), tile_sems.at[half, i]).start()

    copies = [
        pltpu.make_async_copy(left_hbm, left, sems.at[0]),
        pltpu.make_async_copy(right_hbm, right, sems.at[1]),
    ]
    for copy in copies:
        copy.start()
    for half in range(2):
        for i in range(len(halves[half])):
            pltpu.make_async_copy(mine_ref.at[i], place(half, i), tile_sems.at[half, i]).wait()
    for i in range(rank // T):
        for j in range(i):
            tile = gram_left[i * T : (i + 1) * T, j * T : (j + 1) * T]
            gram_left[j * T : (j + 1) * T, i * T : (i + 1) * T] = tile.T
    s = split(sketch[...])
    cross = split(dot_split(split(gram_left[...]), s))
    gram = dot_split(s, cross, ((0,), (0,)))
    for copy in copies:
        copy.wait()
    tall = [
        split(dot(held[...], high, precision=None) + dot(held[...], low, precision=None))
        for held, (high, low) in ((left, s), (right, cross))
    ]
    m = split(inverse_factor(gram))
    left_new_ref[...] = (dot_split(tall[0], m, ((1,), (1,))) * norm).astype(BF16)
    right_new_ref[...] = (dot_split(tall[1], m, ((1,), (1,))) * (1.0 / norm)).astype(BF16)


def truncated(norm, core, mine, theirs, left_core, right_core, target):
    rows, rank = left_core.shape
    out = jax.ShapeDtypeStruct((rows, target), BF16)
    return pl.pallas_call(
        functools.partial(truncate, norm),
        out_shape=(out, out),
        in_specs=[SMEM, ANY, ANY, ANY, ANY],
        out_specs=[VMEM, VMEM],
        scratch_shapes=[
            pltpu.VMEM(left_core.shape, BF16),
            pltpu.VMEM(right_core.shape, BF16),
            pltpu.VMEM((rank, target), F32),
            pltpu.VMEM((rank, rank), F32),
            pltpu.SemaphoreType.DMA((2, mine.shape[0])),
            pltpu.SemaphoreType.DMA((2,)),
        ],
        compiler_params=pltpu.CompilerParams(vmem_limit_bytes=40 << 20),
        name="truncate",
    )(core, mine, theirs, left_core, right_core)


def to_all(x, groups):
    copies = jnp.broadcast_to(x, (len(groups[0]), *x.shape))
    return lax.all_to_all(copies, AXIS, 0, 0, axis_index_groups=groups, tiled=True)


def groups_of(grid):
    first, second, third = grid

    def device(i, j, k, core):
        return ((i * second + j) * third + k) * 2 + core

    scatter = [[device(i, j, k, 0) for j in range(second) for k in range(third)] for i in range(first)]
    scatter += [[device(i, j, k, 1) for i in range(first) for k in range(third)] for j in range(second)]
    exchange = [[device(i, j, k, 0) for i in range(first)] for j in range(second) for k in range(third)]
    exchange += [[device(i, j, k, 1) for j in range(second)] for i in range(first) for k in range(third)]
    return scatter, exchange


def local(left_core, right_core, gauss_core):
    devices = math.prod(CHIPS) * 2
    norm = math.sqrt(left_core.shape[0] * devices)
    core = (lax.axis_index(AXIS) % 2).reshape(1)
    swap = [(i, i ^ 1) for i in range(devices)]
    scatter, exchange = groups_of(CHIPS)
    keep, send = products(core, left_core, right_core, gauss_core)
    x = keep + lax.ppermute(send, AXIS, swap)
    x = x.reshape(len(scatter[0]), -1, 4, T)
    x = lax.all_to_all(x, AXIS, 0, 0, axis_index_groups=scatter, tiled=True).sum(0)
    x = to_all(x, exchange).reshape(-1, *x.shape).sum(0)
    mine = to_all(x, scatter).reshape(keep.shape)
    theirs = lax.ppermute(mine, AXIS, swap)
    return truncated(norm, core, mine, theirs, left_core, right_core, gauss_core.shape[1])


def solution(mesh):
    flat = Mesh(mesh.devices.reshape(-1), (AXIS,))
    spec = P(AXIS, None)
    return jax.shard_map(
        local, mesh=flat, in_specs=(spec, spec, spec), out_specs=(spec, spec), check_vma=False
    )
```

```python
import functools
import math

import jax
import jax.numpy as jnp
from jax import lax
from jax.experimental import pallas as pl
from jax.experimental.pallas import tpu as pltpu
from jax.sharding import Mesh
from jax.sharding import PartitionSpec as P

AXIS = "device"
CHIPS = (8, 8, 4)
HI = lax.Precision.HIGHEST
F32, BF16 = jnp.float32, jnp.bfloat16
T = 128
SUB = 8
OUTER = 32
BESIDE = (1, 4)
TAIL = 1
ANY = pl.BlockSpec(memory_space=pl.ANY)
VMEM = pl.BlockSpec(memory_space=pltpu.VMEM)
SMEM = pl.BlockSpec(memory_space=pltpu.SMEM)


def dot(x, y, dims=((1,), (0,)), precision=HI):
    return lax.dot_general(x, y, (dims, ((), ())), precision=precision, preferred_element_type=F32)


def tiles_of(rank, target):
    sketch = [("s", i, j) for j in range(target // T) for i in range(rank // T)]
    gram = [("g", i, j) for j in range(rank // T) for i in range(j, rank // T)]
    both = sketch + gram
    return both[: len(both) // 2], both[len(both) // 2 :]


def local_products(given, core_ref, left_hbm, right_hbm, gauss_hbm, out_ref, left, right, gauss, sems):
    rank, target = right.shape[1], gauss.shape[1]
    halves = tiles_of(rank, target)

    def put(half, kind, col, value, first):
        for i in range(value.shape[0] // T):
            if (kind, first + i, col) in halves[half]:
                out_ref[halves[half].index((kind, first + i, col))] = value[i * T : (i + 1) * T, :]

    def sketch_half():
        corner = left.at[:, pl.ds(0, T)]
        copies = [
            pltpu.make_async_copy(right_hbm, right, sems.at[0]),
            pltpu.make_async_copy(gauss_hbm, gauss, sems.at[1]),
            pltpu.make_async_copy(left_hbm.at[:, pl.ds(0, T)], corner, sems.at[2]),
        ]
        for copy in copies:
            copy.start()
        for copy in copies:
            copy.wait()
        x = dot(right[...], gauss[...], ((0,), (0,)), None)
        for j in range(target // T):
            put(0, "s", j, x[:, j * T : (j + 1) * T], 0)
        put(0, "g", 0, dot(corner[...], corner[...], ((0,), (0,)), None), 0)

    def gram_half():
        copy = pltpu.make_async_copy(left_hbm, left, sems.at[0])
        copy.start()
        copy.wait()
        for j in range(0, rank // T, 2):
            y = dot(left[:, j * T :], left[:, j * T : (j + 2) * T], ((0,), (0,)), None)
            put(1, "g", j, y[:, :T], j)
            put(1, "g", j + 1, y[T:, T:], j + 1)

    pl.when(core_ref[0] == given)(sketch_half)
    pl.when(core_ref[0] != given)(gram_half)


def products(given, core, left_core, right_core, gauss_core):
    rows, rank = left_core.shape
    target = gauss_core.shape[1]
    return pl.pallas_call(
        functools.partial(local_products, given),
        out_shape=pltpu.VMEM((len(tiles_of(rank, target)[0]), T, T), F32),
        in_specs=[SMEM, ANY, ANY, ANY],
        out_specs=VMEM,
        scratch_shapes=[
            pltpu.VMEM(left_core.shape, BF16),
            pltpu.VMEM(right_core.shape, BF16),
            pltpu.VMEM(gauss_core.shape, BF16),
            pltpu.SemaphoreType.DMA((3,)),
        ],
        cost_estimate=pl.CostEstimate(
            flops=2 * rows * rank * target, bytes_accessed=3 * rows * rank, transcendentals=0
        ),
        name=f"products_{given}",
    )(core, left_core, right_core, gauss_core)


def lane_of(x, c):
    x = x[c // T]
    return jnp.take_along_axis(x, jnp.full(x.shape, c % T, jnp.int32), axis=1)


def row_of(x, k):
    return lax.broadcast_in_dim(x[k : k + 1, :], x.shape, (0, 1))


def tree_sum(terms):
    while len(terms) > 1:
        rest = terms[len(terms) // 2 * 2 :]
        terms = [x + y for x, y in zip(terms[::2], terms[1::2])] + rest
    return terms[0]


def split(x):
    high = x.astype(BF16)
    return high, (x - high.astype(F32)).astype(BF16)


def dot_split(x, y, dims=((1,), (0,))):
    (xh, xl), (yh, yl) = x, y
    return dot(xh, yh, dims, None) + (dot(xh, yl, dims, None) + dot(xl, yh, dims, None))


def inverse_factor(a, beside):
    n = a.shape[0]
    parts = range(n // T)
    sub = lax.broadcasted_iota(jnp.int32, (SUB, T), 0)
    lanes = [lax.broadcasted_iota(jnp.int32, (SUB, T), 1) + T * h for h in parts]
    done = []
    for first in range(0, n, OUTER):
        beside(first // OUTER)
        block = a[first : first + OUTER, :]
        if first:
            u = jnp.concatenate(done, 0)
            row = lax.broadcasted_iota(jnp.int32, u.shape, 0)
            col = lax.broadcasted_iota(jnp.int32, u.shape, 1)
            x = dot_split(
                split(u[:, first : first + OUTER]),
                split(jnp.where((col <= row) | (col >= first), u, 0.0)),
                ((0,), (0,)),
            )
            col = lax.broadcasted_iota(jnp.int32, block.shape, 1)
            block = jnp.where(col >= first, block, 0.0) - x
        rows = [
            [block[i : i + SUB, T * h : T * (h + 1)] for h in parts] for i in range(0, OUTER, SUB)
        ]
        for s in range(OUTER // SUB):
            base = first + SUB * s
            here_part = base // T
            lane = lanes[here_part]
            own = (lane >= base) & (lane < base + SUB)
            w = list(rows[s])
            cols = [lane_of(w, base + k) for k in range(SUB)]
            w[here_part] = jnp.where(
                own, jnp.where(lane == sub + base, 1.0, 0.0), w[here_part]
            )
            f = [jnp.zeros((SUB, T), F32)] * len(w)
            pivot = row_of(cols[0], 0)
            for k in range(SUB):
                here = sub == k
                inverse, root = 1.0 / pivot, lax.rsqrt(pivot)
                for j in range(k + 1, SUB):
                    r = row_of(cols[j], k)
                    if j == k + 1:
                        rest = cols[j] - (cols[k] * r) * inverse
                        pivot = row_of(rest, j)
                        cols[j] = jnp.where(here, r * inverse, rest)
                    else:
                        t = r * inverse
                        cols[j] = jnp.where(here, t, cols[j] - cols[k] * t)
                for h in parts:
                    r = row_of(w[h], k)
                    f[h] = jnp.where(here, r * root, f[h])
                    t = r * inverse
                    w[h] = jnp.where(here, t, w[h] - cols[k] * t)
            keep = [(lanes[h] <= sub + base) | (lanes[h] >= first + OUTER) for h in parts]
            done.append(jnp.concatenate([jnp.where(keep[h], f[h], 0.0) for h in parts], 1))
            ws = [[row_of(w[h], k) for k in range(SUB)] for h in parts]
            for i in range(s + 1, OUTER // SUB):
                m = [lane_of(rows[i], base + k) for k in range(SUB)]
                r = list(rows[i])
                r[here_part] = jnp.where(own, 0.0, r[here_part])
                rows[i] = [r[h] - tree_sum([x * y for x, y in zip(m, ws[h])]) for h in parts]
    m = jnp.concatenate(done, 0)
    row = lax.broadcasted_iota(jnp.int32, m.shape, 0)
    col = lax.broadcasted_iota(jnp.int32, m.shape, 1)
    return jnp.where(row >= col, m, 0.0)


def truncate(norm, core_ref, mine_ref, theirs_ref, left_hbm, right_hbm, left_new_hbm, right_new_hbm,
             left, right, sketch, gram_left, left_out, right_out,
             tile_sems, sems, out_sems):
    rank, target = sketch.shape
    halves = tiles_of(rank, target)
    core = core_ref[0]

    def place(half, i):
        kind, row, col = halves[half][i]
        ref = sketch if kind == "s" else gram_left
        return ref.at[pl.ds(row * T, T), pl.ds(col * T, T)]

    for own in range(2):

        @pl.when(core == own)
        def _():
            for half in range(2):
                src = mine_ref if half == own else theirs_ref
                for i in range(len(halves[half])):
                    pltpu.make_async_copy(src.at[i], place(half, i), tile_sems.at[half, i]).start()

    copies = [
        pltpu.make_async_copy(left_hbm, left, sems.at[0]),
        pltpu.make_async_copy(right_hbm, right, sems.at[1]),
    ]
    for copy in copies:
        copy.start()
    for half in range(2):
        for i in range(len(halves[half])):
            pltpu.make_async_copy(mine_ref.at[i], place(half, i), tile_sems.at[half, i]).wait()
    for i in range(rank // T):
        for j in range(i):
            tile = gram_left[i * T : (i + 1) * T, j * T : (j + 1) * T]
            gram_left[j * T : (j + 1) * T, i * T : (i + 1) * T] = tile.T
    s = split(sketch[...])
    cross = split(dot_split(split(gram_left[...]), s))
    gram = dot_split(s, cross, ((0,), (0,)))
    for copy in copies:
        copy.wait()
    tall = []

    def beside(step):
        for held, (high, low), when in ((left, s, BESIDE[0]), (right, cross, BESIDE[1])):
            if step == when:
                x = held[...]
                tall.append(split(dot(x, high, precision=None) + dot(x, low, precision=None)))

    m = split(inverse_factor(gram, beside))
    chunk_out = left.shape[0] // TAIL
    outs = []
    for scale, (heads, rests), staged, out_hbm in (
        (norm, tall[0], left_out, left_new_hbm),
        (1.0 / norm, tall[1], right_out, right_new_hbm),
    ):
        for part in range(TAIL):
            at = pl.ds(part * chunk_out, chunk_out)
            rows = slice(part * chunk_out, (part + 1) * chunk_out)
            x = dot_split((heads[rows, :], rests[rows, :]), m, ((1,), (1,)))
            staged[at, :] = (x * scale).astype(BF16)
            out = pltpu.make_async_copy(staged.at[at, :], out_hbm.at[at, :], out_sems.at[len(outs)])
            out.start()
            outs.append(out)
    for out in outs:
        out.wait()


def truncated(norm, core, mine, theirs, left_core, right_core, target):
    rows, rank = left_core.shape
    out = jax.ShapeDtypeStruct((rows, target), BF16)
    return pl.pallas_call(
        functools.partial(truncate, norm),
        out_shape=(out, out),
        in_specs=[SMEM, ANY, ANY, ANY, ANY],
        out_specs=[ANY, ANY],
        scratch_shapes=[
            pltpu.VMEM(left_core.shape, BF16),
            pltpu.VMEM(right_core.shape, BF16),
            pltpu.VMEM((rank, target), F32),
            pltpu.VMEM((rank, rank), F32),
            *[pltpu.VMEM((rows, target), BF16)] * 2,
            pltpu.SemaphoreType.DMA((2, mine.shape[0])),
            pltpu.SemaphoreType.DMA((2,)),
            pltpu.SemaphoreType.DMA((2 * TAIL,)),
        ],
        compiler_params=pltpu.CompilerParams(vmem_limit_bytes=40 << 20),
        name="truncate",
    )(core, mine, theirs, left_core, right_core)


def to_all(x, groups):
    copies = jnp.broadcast_to(x, (len(groups[0]), *x.shape))
    return lax.all_to_all(copies, AXIS, 0, 0, axis_index_groups=groups, tiled=True)


def groups_of(grid):
    first, second, third = grid

    def device(i, j, k, core):
        return ((i * second + j) * third + k) * 2 + core

    scatter = [[device(i, j, k, 0) for j in range(second) for k in range(third)] for i in range(first)]
    scatter += [[device(i, j, k, 1) for i in range(first) for k in range(third)] for j in range(second)]
    exchange = [[device(i, j, k, 0) for i in range(first)] for j in range(second) for k in range(third)]
    exchange += [[device(i, j, k, 1) for j in range(second)] for i in range(first) for k in range(third)]
    return scatter, exchange


def local(left_core, right_core, gauss_core):
    devices = math.prod(CHIPS) * 2
    norm = math.sqrt(left_core.shape[0] * devices)
    core = (lax.axis_index(AXIS) % 2).reshape(1)
    swap = [(i, i ^ 1) for i in range(devices)]
    scatter, exchange = groups_of(CHIPS)
    theirs = lax.ppermute(products(1, core, left_core, right_core, gauss_core), AXIS, swap)
    keep = products(0, core, left_core, right_core, gauss_core)
    x = keep + theirs
    x = x.reshape(len(scatter[0]), -1, 4, T)
    x = lax.all_to_all(x, AXIS, 0, 0, axis_index_groups=scatter, tiled=True).sum(0)
    x = to_all(x, exchange).reshape(-1, *x.shape).sum(0)
    mine = to_all(x, scatter).reshape(keep.shape)
    theirs = lax.ppermute(mine, AXIS, swap)
    return truncated(norm, core, mine, theirs, left_core, right_core, gauss_core.shape[1])


def solution(mesh):
    flat = Mesh(mesh.devices.reshape(-1), (AXIS,))
    spec = P(AXIS, None)
    return jax.shard_map(
        local, mesh=flat, in_specs=(spec, spec, spec), out_specs=(spec, spec), check_vma=False
    )
```

```python
import functools
import math

import jax
import jax.numpy as jnp
from jax import lax
from jax.experimental import pallas as pl
from jax.experimental.pallas import tpu as pltpu
from jax.sharding import Mesh
from jax.sharding import PartitionSpec as P

AXIS = "device"
CHIPS = (8, 8, 4)
HI = lax.Precision.HIGHEST
F32, BF16 = jnp.float32, jnp.bfloat16
T = 128
SUB = 8
OUTER = 32
BESIDE = (0, 2)
LATER = (0, 1)
ANY = pl.BlockSpec(memory_space=pl.ANY)
VMEM = pl.BlockSpec(memory_space=pltpu.VMEM)
SMEM = pl.BlockSpec(memory_space=pltpu.SMEM)


def dot(x, y, dims=((1,), (0,)), precision=HI):
    return lax.dot_general(x, y, (dims, ((), ())), precision=precision, preferred_element_type=F32)


def tiles_of(rank, target):
    sketch = [("s", i, j) for j in range(target // T) for i in range(rank // T)]
    gram = [("g", i, j) for j in range(rank // T) for i in range(j, rank // T)]
    both = sketch + gram
    return both[: len(both) // 2], both[len(both) // 2 :]


def local_products(given, core_ref, left_hbm, right_hbm, gauss_hbm, out_ref, left, right, gauss, sems):
    rank, target = right.shape[1], gauss.shape[1]
    halves = tiles_of(rank, target)

    def put(half, kind, col, value, first):
        for i in range(value.shape[0] // T):
            if (kind, first + i, col) in halves[half]:
                out_ref[halves[half].index((kind, first + i, col))] = value[i * T : (i + 1) * T, :]

    def sketch_half():
        corner = left.at[:, pl.ds(0, T)]
        copies = [
            pltpu.make_async_copy(right_hbm, right, sems.at[0]),
            pltpu.make_async_copy(gauss_hbm, gauss, sems.at[1]),
            pltpu.make_async_copy(left_hbm.at[:, pl.ds(0, T)], corner, sems.at[2]),
        ]
        for copy in copies:
            copy.start()
        for copy in copies:
            copy.wait()
        x = dot(right[...], gauss[...], ((0,), (0,)), None)
        for j in range(target // T):
            put(0, "s", j, x[:, j * T : (j + 1) * T], 0)
        put(0, "g", 0, dot(corner[...], corner[...], ((0,), (0,)), None), 0)

    def gram_half():
        copy = pltpu.make_async_copy(left_hbm, left, sems.at[0])
        copy.start()
        copy.wait()
        for j in range(0, rank // T, 2):
            y = dot(left[:, j * T :], left[:, j * T : (j + 2) * T], ((0,), (0,)), None)
            put(1, "g", j, y[:, :T], j)
            put(1, "g", j + 1, y[T:, T:], j + 1)

    pl.when(core_ref[0] == given)(sketch_half)
    pl.when(core_ref[0] != given)(gram_half)


def products(given, core, left_core, right_core, gauss_core):
    rows, rank = left_core.shape
    target = gauss_core.shape[1]
    return pl.pallas_call(
        functools.partial(local_products, given),
        out_shape=pltpu.VMEM((len(tiles_of(rank, target)[0]), T, T), F32),
        in_specs=[SMEM, ANY, ANY, ANY],
        out_specs=VMEM,
        scratch_shapes=[
            pltpu.VMEM(left_core.shape, BF16),
            pltpu.VMEM(right_core.shape, BF16),
            pltpu.VMEM(gauss_core.shape, BF16),
            pltpu.SemaphoreType.DMA((3,)),
        ],
        cost_estimate=pl.CostEstimate(
            flops=2 * rows * rank * target, bytes_accessed=3 * rows * rank, transcendentals=0
        ),
        name=f"products_{given}",
    )(core, left_core, right_core, gauss_core)


def lane_of(x, c):
    x = x[c // T]
    return jnp.take_along_axis(x, jnp.full(x.shape, c % T, jnp.int32), axis=1)


def row_of(x, k):
    return lax.broadcast_in_dim(x[k : k + 1, :], x.shape, (0, 1))


def tree_sum(terms):
    while len(terms) > 1:
        rest = terms[len(terms) // 2 * 2 :]
        terms = [x + y for x, y in zip(terms[::2], terms[1::2])] + rest
    return terms[0]


def split(x):
    high = x.astype(BF16)
    return high, (x - high.astype(F32)).astype(BF16)


def dot_split(x, y, dims=((1,), (0,))):
    (xh, xl), (yh, yl) = x, y
    return dot(xh, yh, dims, None) + (dot(xh, yl, dims, None) + dot(xl, yh, dims, None))


def inverse_factor(a, beside):
    n = a.shape[0]
    parts = range(n // T)
    sub = lax.broadcasted_iota(jnp.int32, (SUB, T), 0)
    lanes = [lax.broadcasted_iota(jnp.int32, (SUB, T), 1) + T * h for h in parts]
    done = []
    for first in range(0, n, OUTER):
        beside(first // OUTER)
        block = a[first : first + OUTER, :]
        if first:
            u = jnp.concatenate(done, 0)
            row = lax.broadcasted_iota(jnp.int32, u.shape, 0)
            col = lax.broadcasted_iota(jnp.int32, u.shape, 1)
            x = dot_split(
                split(u[:, first : first + OUTER]),
                split(jnp.where((col <= row) | (col >= first), u, 0.0)),
                ((0,), (0,)),
            )
            col = lax.broadcasted_iota(jnp.int32, block.shape, 1)
            block = jnp.where(col >= first, block, 0.0) - x
        rows = [
            [block[i : i + SUB, T * h : T * (h + 1)] for h in parts] for i in range(0, OUTER, SUB)
        ]
        for s in range(OUTER // SUB):
            base = first + SUB * s
            here_part = base // T
            lane = lanes[here_part]
            own = (lane >= base) & (lane < base + SUB)
            w = list(rows[s])
            cols = [lane_of(w, base + k) for k in range(SUB)]
            w[here_part] = jnp.where(
                own, jnp.where(lane == sub + base, 1.0, 0.0), w[here_part]
            )
            f = [jnp.zeros((SUB, T), F32)] * len(w)
            pivot = row_of(cols[0], 0)
            for k in range(SUB):
                here = sub == k
                inverse, root = 1.0 / pivot, lax.rsqrt(pivot)
                for j in range(k + 1, SUB):
                    r = row_of(cols[j], k)
                    if j == k + 1:
                        rest = cols[j] - (cols[k] * r) * inverse
                        pivot = row_of(rest, j)
                        cols[j] = jnp.where(here, r * inverse, rest)
                    else:
                        t = r * inverse
                        cols[j] = jnp.where(here, t, cols[j] - cols[k] * t)
                for h in parts:
                    r = row_of(w[h], k)
                    f[h] = jnp.where(here, r * root, f[h])
                    t = r * inverse
                    w[h] = jnp.where(here, t, w[h] - cols[k] * t)
            keep = [(lanes[h] <= sub + base) | (lanes[h] >= first + OUTER) for h in parts]
            done.append(jnp.concatenate([jnp.where(keep[h], f[h], 0.0) for h in parts], 1))
            ws = [[row_of(w[h], k) for k in range(SUB)] for h in parts]
            for i in range(s + 1, OUTER // SUB):
                m = [lane_of(rows[i], base + k) for k in range(SUB)]
                r = list(rows[i])
                r[here_part] = jnp.where(own, 0.0, r[here_part])
                rows[i] = [r[h] - tree_sum([x * y for x, y in zip(m, ws[h])]) for h in parts]
    m = jnp.concatenate(done, 0)
    row = lax.broadcasted_iota(jnp.int32, m.shape, 0)
    col = lax.broadcasted_iota(jnp.int32, m.shape, 1)
    return jnp.where(row >= col, m, 0.0)


def joined(blocks):
    return jnp.concatenate([jnp.concatenate(row, 1) for row in blocks], 0)


def truncate_on(norm, own, mine_ref, theirs_ref, left_hbm, right_hbm, left_new_hbm, right_new_hbm,
             left, right, left_out, right_out, sems, out_sems):
    rank, target = left.shape[1], left_out.shape[1]
    halves = tiles_of(rank, target)
    copies = [
        pltpu.make_async_copy(left_hbm, left, sems.at[0]),
        pltpu.make_async_copy(right_hbm, right, sems.at[1]),
    ]
    for copy in copies:
        copy.start()
    tiles = {
        tile: (mine_ref if half == own else theirs_ref)[i]
        for half in range(2)
        for i, tile in enumerate(halves[half])
    }
    sketch = joined(
        [[tiles["s", i, j] for j in range(target // T)] for i in range(rank // T)]
    )
    gram_left = joined(
        [
            [tiles["g", i, j] if i >= j else tiles["g", j, i].T for j in range(rank // T)]
            for i in range(rank // T)
        ]
    )
    s = split(sketch)
    cross = split(dot_split(split(gram_left), s))
    gram = dot_split(s, cross, ((0,), (0,)))
    for copy in copies:
        copy.wait()
    tall = []

    def beside(step):
        for held, (high, low), when in ((left, s, BESIDE[0]), (right, cross, BESIDE[1])):
            if step == when:
                x = held[...]
                x = dot(x, high, precision=None) + dot(x, low, precision=None)
                tall.append((split(x[:, :T]), x[:, T:]))

    m11 = split(inverse_factor(gram[:T, :T], beside))
    u12 = split(dot_split(m11, split(gram[:T, T:])))
    rest = gram[T:, T:] - dot_split(u12, u12, ((0,), (0,)))
    t = split(dot_split(u12, m11, ((0,), (0,))))
    state = {}

    def later(step):
        for i, (first, second) in enumerate(tall):
            if step == LATER[i]:
                state[i] = (
                    dot_split(first, m11, ((1,), (1,))),
                    split(second - dot_split(first, t, ((1,), (1,)))),
                )

    m22 = split(inverse_factor(rest, later))
    outs = []
    for i, (scale, staged, out_hbm) in enumerate(
        ((norm, left_out, left_new_hbm), (1.0 / norm, right_out, right_new_hbm))
    ):
        early, x = state[i]
        staged[:, :T] = (early * scale).astype(BF16)
        staged[:, T:] = (dot_split(x, m22, ((1,), (1,))) * scale).astype(BF16)
        out = pltpu.make_async_copy(staged, out_hbm, out_sems.at[i])
        out.start()
        outs.append(out)
    for out in outs:
        out.wait()


def truncate(norm, core_ref, *refs):
    for own in range(2):
        pl.when(core_ref[0] == own)(functools.partial(truncate_on, norm, own, *refs))


def truncated(norm, core, mine, theirs, left_core, right_core, target):
    rows, rank = left_core.shape
    out = jax.ShapeDtypeStruct((rows, target), BF16)
    return pl.pallas_call(
        functools.partial(truncate, norm),
        out_shape=(out, out),
        in_specs=[SMEM, VMEM, VMEM, ANY, ANY],
        out_specs=[ANY, ANY],
        scratch_shapes=[
            pltpu.VMEM(left_core.shape, BF16),
            pltpu.VMEM(right_core.shape, BF16),
            *[pltpu.VMEM((rows, target), BF16)] * 2,
            pltpu.SemaphoreType.DMA((2,)),
            pltpu.SemaphoreType.DMA((2,)),
        ],
        compiler_params=pltpu.CompilerParams(vmem_limit_bytes=40 << 20),
        name="truncate",
    )(
        core,
        pltpu.with_memory_space_constraint(mine, pltpu.VMEM),
        pltpu.with_memory_space_constraint(theirs, pltpu.VMEM),
        left_core,
        right_core,
    )


def to_all(x, groups):
    copies = jnp.broadcast_to(x, (len(groups[0]), *x.shape))
    return lax.all_to_all(copies, AXIS, 0, 0, axis_index_groups=groups, tiled=True)


def groups_of(grid):
    first, second, third = grid

    def device(i, j, k, core):
        return ((i * second + j) * third + k) * 2 + core

    scatter = [[device(i, j, k, 0) for j in range(second) for k in range(third)] for i in range(first)]
    scatter += [[device(i, j, k, 1) for i in range(first) for k in range(third)] for j in range(second)]
    exchange = [[device(i, j, k, 0) for i in range(first)] for j in range(second) for k in range(third)]
    exchange += [[device(i, j, k, 1) for j in range(second)] for i in range(first) for k in range(third)]
    return scatter, exchange


def local(left_core, right_core, gauss_core):
    devices = math.prod(CHIPS) * 2
    norm = math.sqrt(left_core.shape[0] * devices)
    core = (lax.axis_index(AXIS) % 2).reshape(1)
    swap = [(i, i ^ 1) for i in range(devices)]
    scatter, exchange = groups_of(CHIPS)
    theirs = lax.ppermute(products(1, core, left_core, right_core, gauss_core), AXIS, swap)
    keep = products(0, core, left_core, right_core, gauss_core)
    x = keep + theirs
    x = x.reshape(len(scatter[0]), -1, 4, T)
    x = lax.all_to_all(x, AXIS, 0, 0, axis_index_groups=scatter, tiled=True).sum(0)
    x = to_all(x, exchange).reshape(-1, *x.shape).sum(0)
    mine = to_all(x, scatter).reshape(keep.shape)
    theirs = lax.ppermute(mine, AXIS, swap)
    return truncated(norm, core, mine, theirs, left_core, right_core, gauss_core.shape[1])


def solution(mesh):
    flat = Mesh(mesh.devices.reshape(-1), (AXIS,))
    spec = P(AXIS, None)
    return jax.shard_map(
        local, mesh=flat, in_specs=(spec, spec, spec), out_specs=(spec, spec), check_vma=False
    )
```

```python
import functools
import math

import jax
import jax.numpy as jnp
from jax import lax
from jax.experimental import pallas as pl
from jax.experimental.pallas import tpu as pltpu
from jax.sharding import Mesh
from jax.sharding import PartitionSpec as P

AXIS = "device"
CHIPS = (8, 8, 4)
HI = lax.Precision.HIGHEST
F32, BF16 = jnp.float32, jnp.bfloat16
T = 128
SUB = 8
OUTER = 32
BESIDE = (0, 2)
LATER = (0, 1)
ANY = pl.BlockSpec(memory_space=pl.ANY)
VMEM = pl.BlockSpec(memory_space=pltpu.VMEM)
SMEM = pl.BlockSpec(memory_space=pltpu.SMEM)


def dot(x, y, dims=((1,), (0,)), precision=HI):
    return lax.dot_general(x, y, (dims, ((), ())), precision=precision, preferred_element_type=F32)


def tiles_of(rank, target):
    sketch = [("s", i, j) for j in range(target // T) for i in range(rank // T)]
    gram = [("g", i, j) for j in range(rank // T) for i in range(j, rank // T)]
    both = sketch + gram
    return both[: len(both) // 2], both[len(both) // 2 :]


def local_products(given, core_ref, left_hbm, right_hbm, gauss_hbm, out_ref, left, right, gauss, sems):
    rank, target = right.shape[1], gauss.shape[1]
    halves = tiles_of(rank, target)

    def put(half, kind, col, value, first):
        for i in range(value.shape[0] // T):
            if (kind, first + i, col) in halves[half]:
                out_ref[halves[half].index((kind, first + i, col))] = value[i * T : (i + 1) * T, :]

    def sketch_half():
        corner = left.at[:, pl.ds(0, T)]
        copies = [
            pltpu.make_async_copy(right_hbm, right, sems.at[0]),
            pltpu.make_async_copy(gauss_hbm, gauss, sems.at[1]),
            pltpu.make_async_copy(left_hbm.at[:, pl.ds(0, T)], corner, sems.at[2]),
        ]
        for copy in copies:
            copy.start()
        for copy in copies:
            copy.wait()
        x = dot(right[...], gauss[...], ((0,), (0,)), None)
        for j in range(target // T):
            put(0, "s", j, x[:, j * T : (j + 1) * T], 0)
        put(0, "g", 0, dot(corner[...], corner[...], ((0,), (0,)), None), 0)

    def gram_half():
        copy = pltpu.make_async_copy(left_hbm, left, sems.at[0])
        copy.start()
        copy.wait()
        for j in range(0, rank // T, 2):
            y = dot(left[:, j * T :], left[:, j * T : (j + 2) * T], ((0,), (0,)), None)
            put(1, "g", j, y[:, :T], j)
            put(1, "g", j + 1, y[T:, T:], j + 1)

    pl.when(core_ref[0] == given)(sketch_half)
    pl.when(core_ref[0] != given)(gram_half)


def products(given, core, left_core, right_core, gauss_core):
    rows, rank = left_core.shape
    target = gauss_core.shape[1]
    return pl.pallas_call(
        functools.partial(local_products, given),
        out_shape=pltpu.VMEM((len(tiles_of(rank, target)[0]), T, T), F32),
        in_specs=[SMEM, ANY, ANY, ANY],
        out_specs=VMEM,
        scratch_shapes=[
            pltpu.VMEM(left_core.shape, BF16),
            pltpu.VMEM(right_core.shape, BF16),
            pltpu.VMEM(gauss_core.shape, BF16),
            pltpu.SemaphoreType.DMA((3,)),
        ],
        cost_estimate=pl.CostEstimate(
            flops=2 * rows * rank * target, bytes_accessed=3 * rows * rank, transcendentals=0
        ),
        name=f"products_{given}",
    )(core, left_core, right_core, gauss_core)


def lane_of(x, c):
    x = x[c // T]
    return jnp.take_along_axis(x, jnp.full(x.shape, c % T, jnp.int32), axis=1)


def row_of(x, k):
    return lax.broadcast_in_dim(x[k : k + 1, :], x.shape, (0, 1))


def tree_sum(terms):
    while len(terms) > 1:
        rest = terms[len(terms) // 2 * 2 :]
        terms = [x + y for x, y in zip(terms[::2], terms[1::2])] + rest
    return terms[0]


def split(x):
    high = x.astype(BF16)
    return high, (x - high.astype(F32)).astype(BF16)


def dot_split(x, y, dims=((1,), (0,))):
    (xh, xl), (yh, yl) = x, y
    return dot(xh, yh, dims, None) + (dot(xh, yl, dims, None) + dot(xl, yh, dims, None))


def inverse_factor(a, beside):
    n = a.shape[0]
    parts = range(n // T)
    sub = lax.broadcasted_iota(jnp.int32, (SUB, T), 0)
    lanes = [lax.broadcasted_iota(jnp.int32, (SUB, T), 1) + T * h for h in parts]
    done = []
    for first in range(0, n, OUTER):
        beside(first // OUTER)
        block = a[first : first + OUTER, :]
        if first:
            u = jnp.concatenate(done, 0)
            row = lax.broadcasted_iota(jnp.int32, u.shape, 0)
            col = lax.broadcasted_iota(jnp.int32, u.shape, 1)
            x = dot_split(
                split(u[:, first : first + OUTER]),
                split(jnp.where((col <= row) | (col >= first), u, 0.0)),
                ((0,), (0,)),
            )
            col = lax.broadcasted_iota(jnp.int32, block.shape, 1)
            block = jnp.where(col >= first, block, 0.0) - x
        rows = [
            [block[i : i + SUB, T * h : T * (h + 1)] for h in parts] for i in range(0, OUTER, SUB)
        ]
        for s in range(OUTER // SUB):
            base = first + SUB * s
            here_part = base // T
            lane = lanes[here_part]
            own = (lane >= base) & (lane < base + SUB)
            w = list(rows[s])
            cols = [lane_of(w, base + k) for k in range(SUB)]
            w[here_part] = jnp.where(
                own, jnp.where(lane == sub + base, 1.0, 0.0), w[here_part]
            )
            f = [jnp.zeros((SUB, T), F32)] * len(w)
            pivot = row_of(cols[0], 0)
            for k in range(SUB):
                here = sub == k
                inverse, root = 1.0 / pivot, lax.rsqrt(pivot)
                for j in range(k + 1, SUB):
                    r = row_of(cols[j], k)
                    if j == k + 1:
                        rest = cols[j] - (cols[k] * r) * inverse
                        pivot = row_of(rest, j)
                        cols[j] = jnp.where(here, r * inverse, rest)
                    else:
                        t = r * inverse
                        cols[j] = jnp.where(here, t, cols[j] - cols[k] * t)
                for h in parts:
                    r = row_of(w[h], k)
                    f[h] = jnp.where(here, r * root, f[h])
                    t = r * inverse
                    w[h] = jnp.where(here, t, w[h] - cols[k] * t)
            keep = [(lanes[h] <= sub + base) | (lanes[h] >= first + OUTER) for h in parts]
            done.append(jnp.concatenate([jnp.where(keep[h], f[h], 0.0) for h in parts], 1))
            ws = [[row_of(w[h], k) for k in range(SUB)] for h in parts]
            for i in range(s + 1, OUTER // SUB):
                m = [lane_of(rows[i], base + k) for k in range(SUB)]
                r = list(rows[i])
                r[here_part] = jnp.where(own, 0.0, r[here_part])
                rows[i] = [r[h] - tree_sum([x * y for x, y in zip(m, ws[h])]) for h in parts]
    m = jnp.concatenate(done, 0)
    row = lax.broadcasted_iota(jnp.int32, m.shape, 0)
    col = lax.broadcasted_iota(jnp.int32, m.shape, 1)
    return jnp.where(row >= col, m, 0.0)


def joined(blocks):
    return jnp.concatenate([jnp.concatenate(row, 1) for row in blocks], 0)


def truncate_on(norm, own, mine_ref, theirs_ref, left, right, left_new_hbm, right_new_hbm,
             left_out, right_out, out_sems):
    rank, target = left.shape[1], left_out.shape[1]
    halves = tiles_of(rank, target)
    tiles = {
        tile: (mine_ref if half == own else theirs_ref)[i]
        for half in range(2)
        for i, tile in enumerate(halves[half])
    }
    sketch = joined(
        [[tiles["s", i, j] for j in range(target // T)] for i in range(rank // T)]
    )
    gram_left = joined(
        [
            [tiles["g", i, j] if i >= j else tiles["g", j, i].T for j in range(rank // T)]
            for i in range(rank // T)
        ]
    )
    s = split(sketch)
    cross = split(dot_split(split(gram_left), s))
    gram = dot_split(s, cross, ((0,), (0,)))
    tall = []

    def beside(step):
        for held, (high, low), when in ((left, s, BESIDE[0]), (right, cross, BESIDE[1])):
            if step == when:
                x = held[...]
                x = dot(x, high, precision=None) + dot(x, low, precision=None)
                tall.append((split(x[:, :T]), x[:, T:]))

    m11 = split(inverse_factor(gram[:T, :T], beside))
    u12 = split(dot_split(m11, split(gram[:T, T:])))
    rest = gram[T:, T:] - dot_split(u12, u12, ((0,), (0,)))
    t = split(dot_split(u12, m11, ((0,), (0,))))
    state = {}

    def later(step):
        for i, (first, second) in enumerate(tall):
            if step == LATER[i]:
                state[i] = (
                    dot_split(first, m11, ((1,), (1,))),
                    split(second - dot_split(first, t, ((1,), (1,)))),
                )

    m22 = split(inverse_factor(rest, later))
    outs = []
    for i, (scale, staged, out_hbm) in enumerate(
        ((norm, left_out, left_new_hbm), (1.0 / norm, right_out, right_new_hbm))
    ):
        early, x = state[i]
        staged[:, :T] = (early * scale).astype(BF16)
        staged[:, T:] = (dot_split(x, m22, ((1,), (1,))) * scale).astype(BF16)
        out = pltpu.make_async_copy(staged, out_hbm, out_sems.at[i])
        out.start()
        outs.append(out)
    for out in outs:
        out.wait()


def truncate(norm, core_ref, *refs):
    for own in range(2):
        pl.when(core_ref[0] == own)(functools.partial(truncate_on, norm, own, *refs))


def truncated(norm, core, mine, theirs, left_core, right_core, target):
    rows, rank = left_core.shape
    out = jax.ShapeDtypeStruct((rows, target), BF16)
    return pl.pallas_call(
        functools.partial(truncate, norm),
        out_shape=(out, out),
        in_specs=[SMEM, VMEM, VMEM, VMEM, VMEM],
        out_specs=[ANY, ANY],
        scratch_shapes=[
            *[pltpu.VMEM((rows, target), BF16)] * 2,
            pltpu.SemaphoreType.DMA((2,)),
        ],
        compiler_params=pltpu.CompilerParams(vmem_limit_bytes=40 << 20),
        name="truncate",
    )(
        core,
        pltpu.with_memory_space_constraint(mine, pltpu.VMEM),
        pltpu.with_memory_space_constraint(theirs, pltpu.VMEM),
        pltpu.with_memory_space_constraint(left_core, pltpu.VMEM),
        pltpu.with_memory_space_constraint(right_core, pltpu.VMEM),
    )


def to_all(x, groups):
    copies = jnp.broadcast_to(x, (len(groups[0]), *x.shape))
    return lax.all_to_all(copies, AXIS, 0, 0, axis_index_groups=groups, tiled=True)


def groups_of(grid):
    first, second, third = grid

    def device(i, j, k, core):
        return ((i * second + j) * third + k) * 2 + core

    scatter = [[device(i, j, k, 0) for j in range(second) for k in range(third)] for i in range(first)]
    scatter += [[device(i, j, k, 1) for i in range(first) for k in range(third)] for j in range(second)]
    exchange = [[device(i, j, k, 0) for i in range(first)] for j in range(second) for k in range(third)]
    exchange += [[device(i, j, k, 1) for j in range(second)] for i in range(first) for k in range(third)]
    return scatter, exchange


def local(left_core, right_core, gauss_core):
    devices = math.prod(CHIPS) * 2
    norm = math.sqrt(left_core.shape[0] * devices)
    core = (lax.axis_index(AXIS) % 2).reshape(1)
    swap = [(i, i ^ 1) for i in range(devices)]
    scatter, exchange = groups_of(CHIPS)
    theirs = lax.ppermute(products(1, core, left_core, right_core, gauss_core), AXIS, swap)
    keep = products(0, core, left_core, right_core, gauss_core)
    x = keep + theirs
    x = x.reshape(len(scatter[0]), -1, 4, T)
    x = lax.all_to_all(x, AXIS, 0, 0, axis_index_groups=scatter, tiled=True).sum(0)
    x = to_all(x, exchange).reshape(-1, *x.shape).sum(0)
    mine = to_all(x, scatter).reshape(keep.shape)
    theirs = lax.ppermute(mine, AXIS, swap)
    return truncated(norm, core, mine, theirs, left_core, right_core, gauss_core.shape[1])


def solution(mesh):
    flat = Mesh(mesh.devices.reshape(-1), (AXIS,))
    spec = P(AXIS, None)
    return jax.shard_map(
        local, mesh=flat, in_specs=(spec, spec, spec), out_specs=(spec, spec), check_vma=False
    )
```
